256 devices in a mesh: ctx: 16 (over z, core), head: 16 (over y, x).
Axes of the slice: x: 4, y: 4, z: 8, core: 2. Of those that a mesh axis runs over, the one named last changes fastest.
Arguments:
- light_query: bfloat16 [32768, 32, 128], P(('ctx', 'head')), may hold values from -6 to 6
- light_keys: bfloat16 [32768, 32, 128], P(('ctx', 'head')), may hold values from -0.5390625 to 0.5390625
- light_values: bfloat16 [32768, 32, 128], P(('ctx', 'head')), may hold values from -6 to 6
- decay_rate: float32 [32], replicated, may hold values from 0.00012207031 to 0.05
- norm_gain: float32 [32, 128], replicated, may hold values from 0.5 to 1.5
- soft_query: bfloat16 [32768, 32, 128], P(('ctx', 'head')), may hold values from -120 to 120
- soft_keys: bfloat16 [32768, 4, 128], P(('ctx', 'head')), may hold values from -8 to 8
- soft_values: bfloat16 [32768, 4, 128], P(('ctx', 'head')), may hold values from -6 to 6
- segment_ids: int32 [32768], P(('ctx', 'head')), may hold values from 0 to 15, never falling along the last dimension, each value on 1 to 4096 neighbouring positions
Outputs:
- light_out: bfloat16 [32768, 32, 128], P(('ctx', 'head'))
- soft_out: bfloat16 [32768, 32, 128], P(('ctx', 'head'))
The draws below stay inside these ranges and needn't reach their ends.
Inputs may be any that keep to these rules, and one draw needn't show every extreme that they name: `segment_ids`: document ids never fall along the tokens; each document covers 1 to 4096 consecutive tokens, and one covers exactly 4096.
All inputs are finite; a program needn't handle non-finite values.
Results may differ from the reference program's by a relative error of at most 0.004.
Values may be sent and summed in bfloat16 or wider, within the bound.
A program may use at most 64 MiB of HBM per device.

```python
import math
import jax
import jax.numpy as jnp
import numpy as np
from jax import lax

HEADS = 32
HD = 128
KVH = 4
GROUP = 2048
TOKENS = 32768
DOC_MOST = 4096
DOCS = 16


def soft_pair(key):
    base = jax.random.fold_in(key, 7001)
    first, second = jax.random.split(base, 2)
    keys_drawn = jnp.clip(jax.random.normal(first, (TOKENS, KVH, HD), jnp.float32), -6.0, 6.0)
    query_drawn = jnp.clip(jax.random.normal(second, (TOKENS, HEADS, HD), jnp.float32), -6.0, 6.0)
    return (query_drawn, keys_drawn)


def draw_soft_query(key, part):
    return soft_pair(key)[0].astype(jnp.bfloat16)


def draw_soft_keys(key, part):
    return soft_pair(key)[1].astype(jnp.bfloat16)


def levels(stream_key, extent, shards, least, top_value):
    loudness, own = 1.0, jax.random.fold_in(stream_key, 6)
    for axis_at, shards_of in shards:
        draws = jnp.exp(jax.random.uniform(jax.random.fold_in(own, axis_at), (shards_of,), jnp.float32, least / len(shards), top_value / len(shards)))
        loudness = loudness * jnp.repeat(draws, extent[axis_at] // shards_of).reshape([-1 if axis == axis_at else 1 for axis in range(len(extent))])
    return loudness


def split_up(number_of, total, most, skew):
    weights = [(1 << 20) // math.isqrt(standing ** skew) + 1 for standing in range(2, number_of + 1)]
    surplus, given = total - most - (number_of - 1), [1] * (number_of - 1)
    while surplus > 0:
        free = [i for i in range(number_of - 1) if given[i] < most]
        whole, remaining = sum([weights[i] for i in free]), surplus
        for i in free:
            more = min(most - given[i], max(1, remaining * weights[i] // whole), surplus)
            given[i] = given[i] + more
            surplus = surplus - more
    return np.array([most] + given)


def uneven_parts(key, amount, total, bound, slope):
    if amount == 2:
        one = jax.random.randint(key, (), max(1, total - bound), min(bound, total - 1) + 1)
        return jnp.stack([one, total - one])
    sizes = jnp.asarray(split_up(amount, total, bound, slope), jnp.int32)
    couples = (amount - 1) // 2
    source_of, sink = sizes[1:1 + 2 * couples:2], sizes[2:2 + 2 * couples:2]
    slack = jnp.minimum(source_of - 1, bound - sink)
    passed = jax.random.randint(jax.random.fold_in(key, 1), (couples,), 0, 1 << 20) % (slack + 1)
    sizes = sizes.at[1:1 + 2 * couples:2].set(source_of - passed).at[2:2 + 2 * couples:2].set(sink + passed)
    return sizes[jax.random.permutation(jax.random.fold_in(key, 2), amount)]


def normal_values(rng, extent, width, most, cuts=(), held_as=jnp.bfloat16):
    drawn = width * jax.random.normal(rng, extent, jnp.float32)
    if cuts:
        drawn = drawn * levels(rng, extent, cuts, -0.22, 0.18)
    return jnp.clip(drawn, -most, most).astype(held_as)


def setup_inputs(seed: int = 0) -> dict:
    keys = jax.random.split(jax.random.key(seed), 10)
    light_query = normal_values(keys[0], (TOKENS, HEADS, HD), 1.0, 6.0, ((0, 256),))
    light_keys = normal_values(keys[1], (TOKENS, HEADS, HD), 0.09, 0.5390625, ((0, 256),))
    light_values = normal_values(keys[2], (TOKENS, HEADS, HD), 1.0, 6.0, ((0, 256),))
    decay_rate = jnp.clip(jnp.exp(jax.random.uniform(keys[3], (HEADS,), jnp.float32, math.log(0.00012207031), math.log(0.05))), 0.00012207031, 0.05)
    norm_gain = jnp.clip(1.0 + 0.1 * jax.random.normal(keys[4], (HEADS, HD), jnp.float32), 0.5, 1.5)
    soft_query = draw_soft_query(jax.random.fold_in(keys[9], 71), 0)
    soft_keys = draw_soft_keys(jax.random.fold_in(keys[9], 71), 0)
    soft_values = normal_values(keys[7], (TOKENS, KVH, HD), 1.0, 6.0, ((0, 256),))
    segment_ids = jnp.searchsorted(jnp.cumsum(uneven_parts(keys[8], DOCS, TOKENS, DOC_MOST, 2)), jnp.arange(TOKENS), side="right").astype(jnp.int32)
    return {"light_query": light_query, "light_keys": light_keys, "light_values": light_values, "decay_rate": decay_rate, "norm_gain": norm_gain, "soft_query": soft_query, "soft_keys": soft_keys, "soft_values": soft_values, "segment_ids": segment_ids}


HIGH = lax.Precision.HIGHEST
NEG_FILL = -1e+30
NORM_EPS = 1e-06

def lightning_core(light_query, light_keys, light_values, decay_rate, segment_ids):
    block = min(512, GROUP)
    blocks = TOKENS // block
    query_blocks = light_query.reshape(blocks, block, HEADS, HD)
    key_blocks = light_keys.reshape(blocks, block, HEADS, HD)
    value_blocks = light_values.reshape(blocks, block, HEADS, HD)
    sid_blocks = segment_ids.reshape(blocks, block)
    offsets = jnp.arange(block, dtype=jnp.int32)
    distance = offsets[:, None] - offsets[None, :]
    causal = distance >= 0
    spread = jnp.maximum(distance, 0).astype(jnp.float32)
    within = jnp.exp(-decay_rate[:, None, None] * spread[None])
    lead_decay = jnp.exp(-decay_rate[None, :] * (offsets + 1).astype(jnp.float32)[:, None])
    tail_decay = jnp.exp(-decay_rate[None, :] * (block - 1 - offsets).astype(jnp.float32)[:, None])
    full_decay = jnp.exp(-decay_rate * block)

    def advance(carried, inputs):
        state_now, prev_sid = carried
        query_block, key_block, value_block, sid_block = inputs
        query_wide = query_block.astype(jnp.float32)
        key_wide = key_block.astype(jnp.float32)
        value_wide = value_block.astype(jnp.float32)
        allowed = causal & (sid_block[:, None] == sid_block[None, :])
        scores = jnp.einsum('thd,jhd->htj', query_wide, key_wide, precision=HIGH)
        weights = scores * jnp.where(allowed[None], within, 0.0)
        local_part = jnp.einsum('htj,jhd->thd', weights, value_wide, precision=HIGH)
        carry_in = (sid_block == prev_sid).astype(jnp.float32)
        inherited = jnp.einsum('thd,hde->the', query_wide, state_now, precision=HIGH)
        inherited = inherited * (lead_decay * carry_in[:, None])[:, :, None]
        last_sid = sid_block[-1]
        keep_rate = jnp.where(last_sid == prev_sid, full_decay, 0.0)
        open_doc = (sid_block == last_sid).astype(jnp.float32)
        weighted_keys = key_wide * (tail_decay * open_doc[:, None])[:, :, None]
        state_next = keep_rate[:, None, None] * state_now + jnp.einsum('jhd,jhe->hde', weighted_keys, value_wide, precision=HIGH)
        return ((state_next, last_sid), local_part + inherited)
    initial = (jnp.zeros((HEADS, HD, HD), jnp.float32), jnp.int32(-1))
    _, outputs = lax.scan(advance, initial, (query_blocks, key_blocks, value_blocks, sid_blocks))
    return outputs.reshape(TOKENS, HEADS, HD)

def softmax_core(soft_query, soft_keys, soft_values, segment_ids):
    tile = min(512, GROUP)
    share = HEADS // KVH
    scale = HD ** (-0.5)
    reach = DOC_MOST
    padded_keys = jnp.concatenate([jnp.zeros((reach, KVH, HD), soft_keys.dtype), soft_keys], 0)
    padded_values = jnp.concatenate([jnp.zeros((reach, KVH, HD), soft_values.dtype), soft_values], 0)
    padded_sids = jnp.concatenate([-jnp.ones((reach,), jnp.int32), segment_ids.astype(jnp.int32)], 0)

    def attend(tile_index):
        start = (tile_index * tile).astype(jnp.int32)
        query_tile = lax.dynamic_slice_in_dim(soft_query, start, tile, 0).astype(jnp.float32).reshape(tile, KVH, share, HD)
        key_tile = lax.dynamic_slice_in_dim(padded_keys, start, reach + tile, 0).astype(jnp.float32)
        value_tile = lax.dynamic_slice_in_dim(padded_values, start, reach + tile, 0).astype(jnp.float32)
        query_sid = lax.dynamic_slice_in_dim(segment_ids.astype(jnp.int32), start, tile, 0)
        key_sid = lax.dynamic_slice_in_dim(padded_sids, start, reach + tile, 0)
        query_pos = start + jnp.arange(tile, dtype=jnp.int32)
        key_pos = start - reach + jnp.arange(reach + tile, dtype=jnp.int32)
        allowed = (key_pos[None, :] <= query_pos[:, None]) & (key_sid[None, :] == query_sid[:, None])
        scores = jnp.einsum('tkgd,jkd->kgtj', query_tile, key_tile, precision=HIGH) * scale
        scores = jnp.where(allowed[None, None], scores, NEG_FILL)
        peak = lax.optimization_barrier(jnp.max(scores, axis=-1, keepdims=True))
        probs = jnp.exp(scores - peak)
        total = lax.optimization_barrier(jnp.sum(probs, axis=-1))
        rounded = lax.optimization_barrier(probs.astype(jnp.bfloat16))
        mixed = jnp.einsum('kgtj,jkd->kgtd', rounded.astype(jnp.float32), value_tile, precision=HIGH)
        mixed = mixed / total[..., None]
        return jnp.transpose(mixed, (2, 0, 1, 3)).reshape(tile, HEADS, HD).astype(jnp.bfloat16)
    tiles = lax.map(attend, jnp.arange(TOKENS // tile, dtype=jnp.int32))
    return tiles.reshape(TOKENS, HEADS, HD)

def reference(light_query, light_keys, light_values, decay_rate, norm_gain, soft_query, soft_keys, soft_values, segment_ids):
    light_raw = lightning_core(light_query, light_keys, light_values, decay_rate, segment_ids)
    mean_square = lax.optimization_barrier(jnp.mean(light_raw * light_raw, axis=-1, keepdims=True))
    light_out = (light_raw * lax.rsqrt(mean_square + NORM_EPS) * norm_gain[None]).astype(jnp.bfloat16)
    soft_out = softmax_core(soft_query, soft_keys, soft_values, segment_ids)
    return (light_out, soft_out)
```

```python
import functools

import jax
import jax.numpy as jnp
from jax import lax
from jax.experimental import pallas as pl
from jax.experimental.pallas import tpu as pltpu
from jax.sharding import PartitionSpec as P

NORM_EPS = 1e-06
FAR = -1e30
BIG = float(2**20)
F32 = jnp.float32
BF16 = jnp.bfloat16
SIDE = 4
MESH = pl.DeviceIdType.MESH


def dot(a, b, dims):
    return lax.dot_general(a, b, (dims, ((), ())), preferred_element_type=F32)


def two_terms(value):
    high = value.astype(BF16)
    low = (value - high.astype(F32)).astype(BF16)
    return high, low


def remote(src, dst, send, recv, **where):
    return pltpu.make_async_remote_copy(
        src_ref=src,
        dst_ref=dst,
        send_sem=send,
        recv_sem=recv,
        device_id=where,
        device_id_type=MESH,
    )


def mix_kernel(
    n_head,
    n_ctx,
    lq,
    lk,
    lv,
    sq,
    kvp,
    seg,
    lam,
    gain,
    light,
    qg,
    kvw,
    st_send,
    st_recv,
    in_send,
    in_recv,
    e_send,
    e_recv,
    loc,
    dist,
    q_ss,
    q_rs,
    y_ss,
    y_rs,
    z_ss,
    z_rs,
    x_ss,
    x_rs,
    p_ss,
    p_rs,
    s_ss,
    s_rs,
    e_ss,
    e_rs,
    b_ss,
    b_rs,
    own_sem,
):
    tok = lq.shape[1]
    hd = lq.shape[2]
    c = lax.axis_index("ctx")
    h = lax.axis_index("head")
    x = lax.rem(h, SIDE)
    y = lax.div(h, SIDE)

    def ctx_at(step):
        return lax.rem(c + step + n_ctx, n_ctx)

    barrier = pltpu.get_barrier_semaphore()
    for i in range(1, n_head):
        pl.semaphore_signal(
            barrier, inc=1, device_id={"head": lax.rem(h + i, n_head)}, device_id_type=MESH
        )
    for step in (1, -1, 2, -2):
        pl.semaphore_signal(barrier, inc=1, device_id={"ctx": ctx_at(step)}, device_id_type=MESH)
    pl.semaphore_wait(barrier, n_head - 1 + 4)

    def y_dev(d):
        return lax.rem(y + d, SIDE) * SIDE + x

    def x_dev(d):
        return y * SIDE + lax.rem(x + d, SIDE)

    def kv_y(d):
        to = lax.rem(y + d, SIDE)
        return remote(kvp.at[to], kvw.at[2, x, y], y_ss.at[d], y_rs.at[d], head=y_dev(d))

    def q_y(d):
        to = lax.rem(y + d, SIDE)
        return remote(sq.at[to], qg.at[y], q_ss.at[d], q_rs.at[d], head=y_dev(d))

    def kv_z():
        return remote(kvw.at[2, x], kvw.at[0, x], z_ss, z_rs, ctx=ctx_at(2))

    def kv_x(slot, which):
        at = slot // 2 * 4 + which
        half = SIDE // 2
        if which == 0:
            piece = kvw.at[slot, x]
            to = 1
        elif which == 1:
            piece = kvw.at[slot, x]
            to = SIDE - 1
        elif which == 2:
            piece = kvw.at[slot, lax.rem(x + SIDE - 1, SIDE), pl.ds(0, half)]
            to = 1
        else:
            piece = kvw.at[slot, lax.rem(x + 1, SIDE), pl.ds(half, half)]
            to = SIDE - 1
        return remote(piece, piece, x_ss.at[at], x_rs.at[at], head=x_dev(to))

    parity = lax.rem(c, 2)

    def kv_pair(d):
        at = lax.rem(x + d, SIDE)
        return remote(
            kvw.at[2 - 2 * parity, at],
            kvw.at[1, at],
            p_ss.at[d],
            p_rs.at[d],
            ctx=c + 1 - 2 * parity,
        )

    for d in range(1, SIDE):
        kv_y(d).start()
    own_kv = pltpu.make_async_copy(kvp.at[y], kvw.at[2, x, y], own_sem.at[0])
    own_kv.start()
    for d in range(1, SIDE):
        q_y(d).start()
    own_q = pltpu.make_async_copy(sq.at[y], qg.at[y], own_sem.at[1])
    own_q.start()

    row = lax.broadcasted_iota(jnp.int32, (tok, tok), 0)
    col = lax.broadcasted_iota(jnp.int32, (tok, tok), 1)
    seg_row = jnp.broadcast_to(seg[...], (tok, tok))
    seg_col = seg_row.T
    first = seg[:, 0:1]
    last = seg[:, tok - 1 : tok]
    dist[0] = jnp.where((row >= col) & (seg_row == seg_col), (col - row).astype(F32), FAR)
    dist[1] = jnp.where(seg_col == last, (row - (tok - 1)).astype(F32), FAR)
    dist[2] = jnp.where(seg_col == first, (-1 - row).astype(F32), FAR)
    edge = jnp.where(
        lax.broadcasted_iota(jnp.int32, (16, hd), 0) < 8,
        jnp.broadcast_to(first, (16, hd)),
        jnp.broadcast_to(last, (16, hd)),
    ).astype(BF16)

    def state_copy(i):
        to = lax.rem(h + i, n_head)
        return remote(st_send.at[to], st_recv.at[h], s_ss.at[i], s_rs.at[i], head=to)

    def make_state(i, carry):
        to = lax.rem(h + i, n_head)
        for a in range(2):
            head = to * 2 + a
            weighted = lk[head].astype(F32) * jnp.exp(lam[pl.ds(head, 1), :] * dist[1])
            high, low = two_terms(weighted)
            values = lv[head]
            state = dot(high, values, ((0,), (0,))) + dot(low, values, ((0,), (0,)))
            st_send[to, a * hd : (a + 1) * hd, :] = state.astype(BF16)
        st_send[to, 2 * hd :, :] = edge

        @pl.when(i >= 2)
        def _():
            state_copy(i - 1).start()

        return carry

    lax.fori_loop(1, n_head + 1, make_state, 0)
    own_state = pltpu.make_async_copy(st_send.at[h], st_recv.at[h], own_sem.at[2])
    own_state.start()

    for d in range(1, SIDE):
        kv_y(d).wait_recv()
    own_kv.wait()
    kv_z().start()
    kv_x(2, 0).start()
    kv_x(2, 1).start()

    def intra(head, carry):
        values = lv[head]
        scores = dot(lq[head], lk[head], ((1,), (1,)))
        high, low = two_terms(scores * jnp.exp(lam[pl.ds(head, 1), :] * dist[0]))
        loc[head] = dot(high, values, ((1,), (0,))) + dot(low, values, ((1,), (0,)))
        return carry

    heads = lq.shape[0]
    lax.fori_loop(0, heads // 2, intra, 0)
    kv_x(2, 0).wait_recv()
    kv_x(2, 1).wait_recv()
    kv_x(2, 2).start()
    kv_x(2, 3).start()
    kv_z().wait_recv()
    kv_x(0, 0).start()
    kv_x(0, 1).start()
    kv_pair(0).start()
    lax.fori_loop(heads // 2, heads, intra, 0)

    def wait_state(i, carry):
        state_copy(i).wait_recv()
        return carry

    lax.fori_loop(1, n_head, wait_state, 0)
    own_state.wait()
    rates = [-lam[pl.ds(h * 2 + a, 1), :] for a in range(2)]
    block_rate = [jnp.exp(r * tok) for r in rates]
    group_rate = [jnp.exp(r * (tok * n_head)) for r in rates]

    def edges_of(b):
        both = st_recv[b, 2 * hd :, :].astype(F32)
        return both[0:1], both[8:9]

    def step_on(b, before, now):
        entry, end = edges_of(b)
        same = (before == end).astype(F32)
        after = tuple(
            st_recv[b, a * hd : (a + 1) * hd, :].astype(F32) + (same * block_rate[a]) * now[a]
            for a in range(2)
        )
        return end, after

    zero = jnp.zeros((hd, hd), F32)
    nobody = jnp.full((1, hd), -1.0, F32)
    end, total = lax.fori_loop(
        0, n_head, lambda b, held: step_on(b, held[0], held[1]), (nobody, (zero, zero))
    )
    for a in range(2):
        e_send[a * hd : (a + 1) * hd, :] = total[a]
    start, _ = edges_of(0)
    e_send[2 * hd :, :] = jnp.where(
        lax.broadcasted_iota(jnp.int32, (8, hd), 0) < 4,
        jnp.broadcast_to(start, (8, hd)),
        jnp.broadcast_to(end, (8, hd)),
    )

    kv_x(0, 0).wait_recv()
    kv_x(0, 1).wait_recv()
    kv_x(0, 2).start()
    kv_x(0, 3).start()
    kv_pair(SIDE - 1).start()
    kv_pair(1).start()

    def e_copy(step):
        return remote(e_send, e_recv.at[step - 1], e_ss.at[step - 1], e_rs.at[step - 1], ctx=ctx_at(step))

    e_copy(1).start()
    e_copy(2).start()
    e_copy(1).wait_recv()
    e_copy(2).wait_recv()

    near = e_recv[0, 2 * hd :, :]
    far = e_recv[1, 2 * hd :, :]
    near_start, near_end, far_end = near[0:1], near[4:5], far[4:5]
    through = ((near_start == near_end) & (near_end == far_end)).astype(F32)
    entering = tuple(
        e_recv[0, a * hd : (a + 1) * hd, :]
        + (through * group_rate[a]) * e_recv[1, a * hd : (a + 1) * hd, :]
        for a in range(2)
    )

    def give(b, held):
        before, now = held
        entry, _ = edges_of(b)
        linked = (before == entry).astype(F32)
        for a in range(2):
            in_send[b, a * hd : (a + 1) * hd, :] = (linked * now[a]).astype(BF16)
        return step_on(b, before, now)

    lax.fori_loop(0, n_head, give, (near_end, entering))

    def in_copy(i):
        to = lax.rem(h + i, n_head)
        return remote(in_send.at[to], in_recv.at[h], b_ss.at[i], b_rs.at[i], head=to)

    def send_in(i, carry):
        in_copy(i).start()
        return carry

    lax.fori_loop(1, n_head, send_in, 0)
    own_in = pltpu.make_async_copy(in_send.at[h], in_recv.at[h], own_sem.at[3])
    own_in.start()

    for slot in (2, 0):
        for which in (2, 3):
            kv_x(slot, which).wait_recv()
    kv_pair(2).start()

    def finish(owner):
        for a in range(2):
            head = owner * 2 + a
            lead = jnp.exp(lam[pl.ds(head, 1), :] * dist[2])
            raw = loc[head] + lead * dot(lq[head], in_recv[owner, a * hd : (a + 1) * hd, :], ((1,), (0,)))
            square = jnp.mean(raw * raw, axis=-1, keepdims=True)
            light[head] = (raw * lax.rsqrt(square + NORM_EPS) * gain[pl.ds(head, 1), :]).astype(BF16)

    own_in.wait()
    finish(h)

    def finish_from(i, carry):
        in_copy(i).wait_recv()
        finish(lax.rem(h + n_head - i, n_head))
        return carry

    lax.fori_loop(1, n_head, finish_from, 0)

    for d in range(1, SIDE):
        q_y(d).wait_recv()
        q_y(d).wait_send()
        kv_y(d).wait_send()
    own_q.wait()
    for d in range(SIDE):
        kv_pair(d).wait_recv()
        kv_pair(d).wait_send()
    kv_z().wait_send()
    for slot in (2, 0):
        for which in range(4):
            kv_x(slot, which).wait_send()
    for step in (1, 2):
        e_copy(step).wait_send()

    def drain(i, carry):
        state_copy(i).wait_send()
        in_copy(i).wait_send()
        return carry

    lax.fori_loop(1, n_head, drain, 0)


def mix(lq, lk, lv, sq, kvp, seg, lam, gain, n_head, n_ctx):
    heads, tok, hd = lq.shape
    rows = sq.shape[1]
    pack = kvp.shape[1]
    dma = pltpu.SemaphoreType.DMA
    vmem = pl.BlockSpec(memory_space=pltpu.VMEM)
    return pl.pallas_call(
        functools.partial(mix_kernel, n_head, n_ctx),
        name="mix",
        out_shape=(
            jax.ShapeDtypeStruct((heads, tok, hd), BF16),
            jax.ShapeDtypeStruct((SIDE, rows, hd), BF16),
            jax.ShapeDtypeStruct((3, SIDE, SIDE, pack, hd), BF16),
        ),
        in_specs=[vmem] * 8,
        out_specs=(vmem, vmem, vmem),
        scratch_shapes=[
            pltpu.VMEM((n_head, 2 * hd + 16, hd), BF16),
            pltpu.VMEM((n_head, 2 * hd + 16, hd), BF16),
            pltpu.VMEM((n_head, 2 * hd, hd), BF16),
            pltpu.VMEM((n_head, 2 * hd, hd), BF16),
            pltpu.VMEM((2 * hd + 8, hd), F32),
            pltpu.VMEM((2, 2 * hd + 8, hd), F32),
            pltpu.VMEM((heads, tok, hd), F32),
            pltpu.VMEM((3, tok, tok), F32),
            dma((SIDE,)),
            dma((SIDE,)),
            dma((SIDE,)),
            dma((SIDE,)),
            dma,
            dma,
            dma((8,)),
            dma((8,)),
            dma((SIDE,)),
            dma((SIDE,)),
            dma((n_head,)),
            dma((n_head,)),
            dma((2,)),
            dma((2,)),
            dma((n_head,)),
            dma((n_head,)),
            dma((4,)),
        ],
        compiler_params=pltpu.CompilerParams(collective_id=0, has_side_effects=True),
    )(lq, lk, lv, sq, kvp, seg, lam, gain)


KEY_BLOCKS = 4
ROWS = 512


def soft_kernel(scale, q_ref, kvw, out, keys, values, ids, tagged, acc, peak):
    groups, side, _, pack, hd = kvw.shape
    rows = q_ref.shape[1]
    tok = hd
    blocks = groups * side * side
    x = lax.rem(lax.axis_index("head"), side)
    docs = lax.broadcasted_iota(jnp.int32, (tok, hd), 0).astype(F32)

    def tags(row):
        return (jnp.broadcast_to(row, (hd, tok)) == docs).astype(F32).T

    lane = lax.broadcasted_iota(jnp.int32, (tok, hd), 1)
    for b in range(KEY_BLOCKS):
        at = pl.ds(b * tok, tok)
        keys[at, 0:hd] = jnp.zeros((tok, hd), BF16)
        keys[at, hd:] = (lane == hd - 1).astype(BF16)
        values[at, 0:hd] = jnp.zeros((tok, hd), BF16)
        values[at, hd:] = jnp.ones((tok, hd), BF16)

    def lay(n, carry):
        g = lax.div(n, side * side)
        yy = lax.rem(lax.div(n, side), side)
        xx = lax.rem(n, side)
        at = pl.ds(pl.multiple_of((n + KEY_BLOCKS) * tok, tok), tok)
        id_row = kvw[g, xx, yy, 2 * tok :, :].astype(F32)[0:1]
        keys[at, 0:hd] = kvw[g, xx, yy, 0:tok, :]
        keys[at, hd:] = tags(id_row).astype(BF16)
        values[at, 0:hd] = kvw[g, xx, yy, tok : 2 * tok, :]
        values[at, hd:] = jnp.ones((tok, hd), BF16)
        ids[pl.ds(n, 1), :] = id_row
        return carry

    lax.fori_loop(0, blocks, lay, 0)
    wide = KEY_BLOCKS * tok
    block_at = lax.broadcasted_iota(jnp.int32, (blocks, tok), 0)
    lane_at = lax.broadcasted_iota(jnp.int32, (blocks, tok), 1)
    tail = lax.broadcasted_iota(jnp.int32, (ROWS, wide), 1) - (wide - tok)
    inner = lax.rem(lax.broadcasted_iota(jnp.int32, (ROWS, wide), 0), tok)
    causal = tail <= inner

    def block(yy, carry):
        n = 2 * side * side + yy * side + x
        id_row = ids[pl.ds(n, 1), :]
        entry = id_row[:, 0:1]
        needed = (ids[...] == entry) & (lane_at == tok - 1) & (block_at < n)
        count = jnp.sum(needed.astype(F32)).astype(jnp.int32)
        tiles = lax.div(count + KEY_BLOCKS, KEY_BLOCKS)
        off = ((1.0 - tags(id_row)) * -BIG).astype(BF16)

        def chunk(r, inner_carry):
            at = pl.ds(pl.multiple_of(r * ROWS, ROWS), ROWS)
            tagged[:, 0:hd] = q_ref[yy, at, :]
            for t in range(ROWS // tok):
                tagged[t * tok : (t + 1) * tok, hd:] = off

            def tile(i, masked):
                low = pl.multiple_of((n + 1 + KEY_BLOCKS - (i + 1) * KEY_BLOCKS) * tok, tok)
                score = dot(tagged[...], keys[pl.ds(low, wide), :], ((1,), (1,)))
                if masked:
                    score = jnp.where(causal, score, -4.0 * BIG)
                    top = jnp.max(score, axis=-1, keepdims=True)
                else:
                    old = peak[...]
                    top = jnp.maximum(old, jnp.max(score, axis=-1, keepdims=True))
                prob = jnp.exp2((score - top) * scale).astype(BF16)
                add = dot(prob, values[pl.ds(low, wide), :], ((1,), (0,)))
                if masked:
                    acc[...] = add
                    peak[...] = top
                else:
                    acc[...] = acc[...] * jnp.exp2((old - top) * scale) + add
                    peak[...] = top

            tile(0, True)

            def later(i, c):
                tile(i, False)
                return c

            lax.fori_loop(1, tiles, later, 0)
            out[yy, at, :] = (acc[:, 0:hd] / acc[:, hd:]).astype(BF16)
            return inner_carry

        return lax.fori_loop(0, rows // ROWS, chunk, carry)

    lax.fori_loop(0, side, block, 0)


def soft(qg, kvw):
    side, rows, hd = qg.shape
    tok = hd
    blocks = kvw.shape[0] * side * side
    vmem = pl.BlockSpec(memory_space=pltpu.VMEM)
    scale = hd ** (-0.5) * 1.4426950408889634
    return pl.pallas_call(
        functools.partial(soft_kernel, scale),
        name="soft",
        out_shape=jax.ShapeDtypeStruct(qg.shape, BF16),
        in_specs=[vmem, vmem],
        out_specs=vmem,
        scratch_shapes=[
            pltpu.VMEM(((blocks + KEY_BLOCKS) * tok, 2 * hd), BF16),
            pltpu.VMEM(((blocks + KEY_BLOCKS) * tok, 2 * hd), BF16),
            pltpu.VMEM((blocks, tok), F32),
            pltpu.VMEM((ROWS, 2 * hd), BF16),
            pltpu.VMEM((ROWS, 2 * hd), F32),
            pltpu.VMEM((ROWS, 1), F32),
        ],
    )(qg, kvw)


def back_kernel(src, dst, ss, rs, own_sem):
    h = lax.axis_index("head")
    x = lax.rem(h, SIDE)
    y = lax.div(h, SIDE)
    barrier = pltpu.get_barrier_semaphore()

    def dev(d):
        return lax.rem(y + d, SIDE) * SIDE + x

    for d in range(1, SIDE):
        pl.semaphore_signal(barrier, inc=1, device_id={"head": dev(d)}, device_id_type=MESH)
    pl.semaphore_wait(barrier, SIDE - 1)

    def copy(d):
        return remote(src.at[lax.rem(y + d, SIDE)], dst.at[y], ss.at[d], rs.at[d], head=dev(d))

    for d in range(1, SIDE):
        copy(d).start()
    own = pltpu.make_async_copy(src.at[y], dst.at[y], own_sem)
    own.start()
    for d in range(1, SIDE):
        copy(d).wait()
    own.wait()


def back(value):
    dma = pltpu.SemaphoreType.DMA
    vmem = pl.BlockSpec(memory_space=pltpu.VMEM)
    return pl.pallas_call(
        back_kernel,
        name="back",
        out_shape=jax.ShapeDtypeStruct(value.shape, value.dtype),
        in_specs=[vmem],
        out_specs=vmem,
        scratch_shapes=[dma((SIDE,)), dma((SIDE,)), dma],
        compiler_params=pltpu.CompilerParams(collective_id=1, has_side_effects=True),
    )(value)


def body(
    light_query,
    light_keys,
    light_values,
    decay_rate,
    norm_gain,
    soft_query,
    soft_keys,
    soft_values,
    segment_ids,
):
    n_head = lax.axis_size("head")
    n_ctx = lax.axis_size("ctx")
    tok, heads, hd = light_query.shape
    kv_heads = soft_keys.shape[1]

    def by_head(value):
        return jnp.transpose(value, (1, 0, 2))

    seg = segment_ids.astype(F32)[None, :]
    id_rows = jnp.broadcast_to(seg.astype(BF16)[None], (kv_heads, 16, tok))
    kvp = jnp.concatenate([by_head(soft_keys), by_head(soft_values), id_rows], axis=1)
    lam = jnp.broadcast_to(decay_rate[:, None], (heads, hd))
    sq = by_head(soft_query).reshape(kv_heads, heads // kv_heads * tok, hd)
    light, qg, kvw = mix(
        by_head(light_query),
        by_head(light_keys),
        by_head(light_values),
        sq,
        kvp,
        seg,
        lam,
        norm_gain,
        n_head,
        n_ctx,
    )
    out = back(soft(qg, kvw)).reshape(heads, tok, hd)
    return (by_head(light), by_head(out))


def solution(mesh):
    wide = P(("ctx", "head"), None, None)
    return jax.shard_map(
        body,
        mesh=mesh,
        in_specs=(wide, wide, wide, P(), P(), wide, wide, wide, P(("ctx", "head"))),
        out_specs=(wide, wide),
        check_vma=False,
    )
```

```python
import functools

import jax
import jax.numpy as jnp
from jax import lax
from jax.experimental import pallas as pl
from jax.experimental.pallas import tpu as pltpu
from jax.sharding import PartitionSpec as P

NORM_EPS = 1e-06
FAR = -1e30
BIG = float(2**20)
F32 = jnp.float32
BF16 = jnp.bfloat16
SIDE = 4
KEY_BLOCKS = 4
ROWS = 512
ONES = 16
MESH = pl.DeviceIdType.MESH


def dot(a, b, dims):
    return lax.dot_general(a, b, (dims, ((), ())), preferred_element_type=F32)


def two_terms(value):
    high = value.astype(BF16)
    low = (value - high.astype(F32)).astype(BF16)
    return high, low


def remote(src, dst, send, recv, **where):
    return pltpu.make_async_remote_copy(
        src_ref=src,
        dst_ref=dst,
        send_sem=send,
        recv_sem=recv,
        device_id=where,
        device_id_type=MESH,
    )


def mix_kernel(
    n_head,
    n_ctx,
    scale,
    lq,
    lk,
    lv,
    sq,
    kvp,
    seg,
    lam,
    gain,
    light,
    out,
    qg,
    kvw,
    so,
    keys,
    values,
    tagged,
    acc,
    score_d,
    score_a,
    score_b,
    prob_a,
    prob_b,
    st_send,
    st_recv,
    in_send,
    in_recv,
    e_send,
    e_recv,
    loc,
    dist,
    q_ss,
    q_rs,
    y_ss,
    y_rs,
    z_ss,
    z_rs,
    x_ss,
    x_rs,
    p_ss,
    p_rs,
    s_ss,
    s_rs,
    e_ss,
    e_rs,
    b_ss,
    b_rs,
    o_ss,
    o_rs,
    own_sem,
):
    tok = lq.shape[1]
    hd = lq.shape[2]
    c = lax.axis_index("ctx")
    h = lax.axis_index("head")
    x = lax.rem(h, SIDE)
    y = lax.div(h, SIDE)

    def ctx_at(step):
        return lax.rem(c + step + n_ctx, n_ctx)

    barrier = pltpu.get_barrier_semaphore()
    for i in range(1, n_head):
        pl.semaphore_signal(
            barrier, inc=1, device_id={"head": lax.rem(h + i, n_head)}, device_id_type=MESH
        )
    for step in (1, -1, 2, -2):
        pl.semaphore_signal(barrier, inc=1, device_id={"ctx": ctx_at(step)}, device_id_type=MESH)
    pl.semaphore_wait(barrier, n_head - 1 + 4)

    def y_dev(d):
        return lax.rem(y + d, SIDE) * SIDE + x

    def x_dev(d):
        return y * SIDE + lax.rem(x + d, SIDE)

    def kv_y(d):
        to = lax.rem(y + d, SIDE)
        return remote(kvp.at[to], kvw.at[2, x, y], y_ss.at[d], y_rs.at[d], head=y_dev(d))

    def q_y(d):
        to = lax.rem(y + d, SIDE)
        return remote(sq.at[to], qg.at[y], q_ss.at[d], q_rs.at[d], head=y_dev(d))

    def kv_z():
        return remote(kvw.at[2, x], kvw.at[0, x], z_ss, z_rs, ctx=ctx_at(2))

    def kv_x(slot, which):
        at = slot // 2 * 4 + which
        half = SIDE // 2
        if which == 0:
            piece = kvw.at[slot, x]
            to = 1
        elif which == 1:
            piece = kvw.at[slot, x]
            to = SIDE - 1
        elif which == 2:
            piece = kvw.at[slot, lax.rem(x + SIDE - 1, SIDE), pl.ds(0, half)]
            to = 1
        else:
            piece = kvw.at[slot, lax.rem(x + 1, SIDE), pl.ds(half, half)]
            to = SIDE - 1
        return remote(piece, piece, x_ss.at[at], x_rs.at[at], head=x_dev(to))

    parity = lax.rem(c, 2)

    def kv_pair(d):
        at = lax.rem(x + d, SIDE)
        return remote(
            kvw.at[2 - 2 * parity, at],
            kvw.at[1, at],
            p_ss.at[d],
            p_rs.at[d],
            ctx=c + 1 - 2 * parity,
        )

    for d in range(1, SIDE):
        kv_y(d).start()
    own_kv = pltpu.make_async_copy(kvp.at[y], kvw.at[2, x, y], own_sem.at[0])
    own_kv.start()
    for d in range(1, SIDE):
        q_y(d).start()
    own_q = pltpu.make_async_copy(sq.at[y], qg.at[y], own_sem.at[1])
    own_q.start()

    row = lax.broadcasted_iota(jnp.int32, (tok, tok), 0)
    col = lax.broadcasted_iota(jnp.int32, (tok, tok), 1)
    seg_row = jnp.broadcast_to(seg[...], (tok, tok))
    seg_col = seg_row.T
    first = seg[:, 0:1]
    last = seg[:, tok - 1 : tok]
    dist[0] = jnp.where((row >= col) & (seg_row == seg_col), (col - row).astype(F32), FAR)
    dist[1] = jnp.where(seg_col == last, (row - (tok - 1)).astype(F32), FAR)
    dist[2] = jnp.where(seg_col == first, (-1 - row).astype(F32), FAR)
    edge = jnp.where(
        lax.broadcasted_iota(jnp.int32, (16, hd), 0) < 8,
        jnp.broadcast_to(first, (16, hd)),
        jnp.broadcast_to(last, (16, hd)),
    ).astype(BF16)

    def state_copy(i):
        to = lax.rem(h + i, n_head)
        return remote(st_send.at[to], st_recv.at[h], s_ss.at[i], s_rs.at[i], head=to)

    def make_state(i, carry):
        to = lax.rem(h + i, n_head)
        for a in range(2):
            head = to * 2 + a
            weighted = lk[head].astype(F32) * jnp.exp(lam[pl.ds(head, 1), :] * dist[1])
            high, low = two_terms(weighted)
            values = lv[head]
            state = dot(high, values, ((0,), (0,))) + dot(low, values, ((0,), (0,)))
            st_send[to, a * hd : (a + 1) * hd, :] = state.astype(BF16)
        st_send[to, 2 * hd :, :] = edge

        @pl.when(i >= 2)
        def _():
            state_copy(i - 1).start()

        return carry

    lax.fori_loop(1, n_head + 1, make_state, 0)
    own_state = pltpu.make_async_copy(st_send.at[h], st_recv.at[h], own_sem.at[2])
    own_state.start()

    for d in range(1, SIDE):
        kv_y(d).wait_recv()
    own_kv.wait()
    kv_z().start()
    kv_x(2, 0).start()
    kv_x(2, 1).start()

    def intra(head, carry):
        values = lv[head]
        scores = dot(lq[head], lk[head], ((1,), (1,)))
        high, low = two_terms(scores * jnp.exp(lam[pl.ds(head, 1), :] * dist[0]))
        loc[head] = dot(high, values, ((1,), (0,))) + dot(low, values, ((1,), (0,)))
        return carry

    heads = lq.shape[0]
    lax.fori_loop(0, heads // 2, intra, 0)
    kv_x(2, 0).wait_recv()
    kv_x(2, 1).wait_recv()
    kv_x(2, 2).start()
    kv_x(2, 3).start()
    kv_z().wait_recv()
    kv_x(0, 0).start()
    kv_x(0, 1).start()
    kv_pair(0).start()
    lax.fori_loop(heads // 2, heads, intra, 0)

    def wait_state(i, carry):
        state_copy(i).wait_recv()
        return carry

    lax.fori_loop(1, n_head, wait_state, 0)
    own_state.wait()
    rates = [-lam[pl.ds(h * 2 + a, 1), :] for a in range(2)]
    block_rate = [jnp.exp(r * tok) for r in rates]
    group_rate = [jnp.exp(r * (tok * n_head)) for r in rates]

    def edges_of(b):
        both = st_recv[b, 2 * hd :, :].astype(F32)
        return both[0:1], both[8:9]

    def step_on(b, before, now):
        entry, end = edges_of(b)
        same = (before == end).astype(F32)
        after = tuple(
            st_recv[b, a * hd : (a + 1) * hd, :].astype(F32) + (same * block_rate[a]) * now[a]
            for a in range(2)
        )
        return end, after

    zero = jnp.zeros((hd, hd), F32)
    nobody = jnp.full((1, hd), -1.0, F32)
    end, total = lax.fori_loop(
        0, n_head, lambda b, held: step_on(b, held[0], held[1]), (nobody, (zero, zero))
    )
    for a in range(2):
        e_send[a * hd : (a + 1) * hd, :] = total[a]
    start, _ = edges_of(0)
    e_send[2 * hd :, :] = jnp.where(
        lax.broadcasted_iota(jnp.int32, (8, hd), 0) < 4,
        jnp.broadcast_to(start, (8, hd)),
        jnp.broadcast_to(end, (8, hd)),
    )

    kv_x(0, 0).wait_recv()
    kv_x(0, 1).wait_recv()
    kv_x(0, 2).start()
    kv_x(0, 3).start()
    kv_pair(SIDE - 1).start()
    kv_pair(1).start()

    def e_copy(step):
        return remote(e_send, e_recv.at[step - 1], e_ss.at[step - 1], e_rs.at[step - 1], ctx=ctx_at(step))

    e_copy(1).start()
    e_copy(2).start()
    side = SIDE
    wide = KEY_BLOCKS * tok
    docs = lax.broadcasted_iota(jnp.int32, (hd, tok), 0).astype(F32)

    def tags(id_row):
        return (jnp.broadcast_to(id_row, (hd, tok)) == docs).astype(F32).T

    def lay(g):
        def lay_row(yy, carry):
            for xx in range(side):
                n = (g * side + yy) * side + xx
                at = pl.ds(pl.multiple_of(n * tok, tok), tok)
                id_row = kvw[g, xx, yy, 2 * tok :, :].astype(F32)[0:1]
                keys[at, 0:hd] = kvw[g, xx, yy, 0:tok, :]
                keys[at, hd:] = tags(id_row).astype(BF16)
                values[n, 0:hd, :] = kvw[g, xx, yy, tok : 2 * tok, :]
                values[n, hd:, :] = jnp.ones((ONES, tok), BF16)
            return carry

        lax.fori_loop(0, side, lay_row, 0)

    blocks = 3 * side * side
    for b in range(KEY_BLOCKS - 1):
        values[blocks + b] = jnp.zeros((hd + ONES, tok), BF16)
    acc[...] = jnp.zeros(acc.shape, F32)

    kv_x(2, 2).wait_recv()
    kv_x(2, 3).wait_recv()
    lay(2)
    kv_x(0, 2).wait_recv()
    kv_x(0, 3).wait_recv()
    kv_pair(2).start()
    lay(0)

    e_copy(1).wait_recv()
    e_copy(2).wait_recv()

    near = e_recv[0, 2 * hd :, :]
    far = e_recv[1, 2 * hd :, :]
    near_start, near_end, far_end = near[0:1], near[4:5], far[4:5]
    through = ((near_start == near_end) & (near_end == far_end)).astype(F32)
    entering = tuple(
        e_recv[0, a * hd : (a + 1) * hd, :]
        + (through * group_rate[a]) * e_recv[1, a * hd : (a + 1) * hd, :]
        for a in range(2)
    )

    def give(b, held):
        before, now = held
        entry, _ = edges_of(b)
        linked = (before == entry).astype(F32)
        for a in range(2):
            in_send[b, a * hd : (a + 1) * hd, :] = (linked * now[a]).astype(BF16)
        return step_on(b, before, now)

    lax.fori_loop(0, n_head, give, (near_end, entering))

    def in_copy(i):
        to = lax.rem(h + i, n_head)
        return remote(in_send.at[to], in_recv.at[h], b_ss.at[i], b_rs.at[i], head=to)

    def send_in(i, carry):
        in_copy(i).start()
        return carry

    lax.fori_loop(1, n_head, send_in, 0)
    own_in = pltpu.make_async_copy(in_send.at[h], in_recv.at[h], own_sem.at[3])
    own_in.start()

    for d in range(SIDE):
        kv_pair(d).wait_recv()
    lay(1)
    for d in range(1, SIDE):
        q_y(d).wait_recv()
    own_q.wait()

    later_key = lax.broadcasted_iota(jnp.int32, (tok, ROWS), 0) > lax.rem(
        lax.broadcasted_iota(jnp.int32, (tok, ROWS), 1), tok
    )
    rows = qg.shape[1]
    key_tiles = 2 * side * side // KEY_BLOCKS
    prob_b[tok:, :] = jnp.zeros((wide - tok, ROWS), BF16)

    def o_copy(s):
        to = lax.rem(y + s, SIDE)
        return remote(so.at[to], out.at[y], o_ss.at[s], o_rs.at[s], head=y_dev(s))

    def attend(s, carry):
        yy = lax.rem(y + s, SIDE)
        n = 2 * side * side + yy * side + x
        id_row = kvw[2, x, yy, 2 * tok :, :].astype(F32)[0:1]
        off = ((1.0 - tags(id_row)) * -BIG).astype(BF16)

        def first_block(i):
            return jnp.maximum(n - (i + 1) * KEY_BLOCKS, 0)

        def score(i):
            low = pl.multiple_of(first_block(i) * tok, tok)
            return dot(keys[pl.ds(low, wide), :], tagged[...], ((1,), (1,)))

        def soften(src, dst, peak):
            top = jnp.maximum(peak, jnp.max(src[...], axis=0, keepdims=True))
            dst[...] = jnp.exp2((src[...] - top) * scale).astype(BF16)
            return top, jnp.exp2((peak - top) * scale)

        def gather(i, prob, fade):
            low = first_block(i)
            tile = jnp.concatenate([values[low + j] for j in range(KEY_BLOCKS)], axis=1)
            acc[...] = acc[...] * fade + dot(tile, prob[...], ((1,), (0,)))

        def chunk(r, inner):
            at = pl.ds(pl.multiple_of(r * ROWS, ROWS), ROWS)
            tagged[:, 0:hd] = qg[yy, at, :]
            for t in range(ROWS // tok):
                tagged[t * tok : (t + 1) * tok, hd:] = off
            diagonal = pl.ds(pl.multiple_of(n * tok, tok), tok)
            own_scores = dot(keys[diagonal, :], tagged[...], ((1,), (1,)))
            score_d[...] = jnp.where(later_key, -4.0 * BIG, own_scores)
            score_a[...] = score(0)
            prob_b[tok:, :] = jnp.zeros((wide - tok, ROWS), BF16)
            peak = jnp.max(score_d[...], axis=0, keepdims=True)
            prob_b[0:tok, :] = jnp.exp2((score_d[...] - peak) * scale).astype(BF16)

            def pair(p, held):
                peak, fade = held
                i = p * 2
                score_b[...] = score(i + 1)
                gather(i - 1, prob_b, fade)
                peak, fade = soften(score_a, prob_a, peak)
                score_a[...] = score(i + 2)
                gather(i, prob_a, fade)
                return soften(score_b, prob_b, peak)

            start = (peak, jnp.zeros((1, ROWS), F32))
            _, fade = lax.fori_loop(0, key_tiles // 2, pair, start)
            gather(key_tiles - 1, prob_b, fade)
            result = acc[0:hd, :] / acc[hd : hd + 1, :]
            for t in range(ROWS // tok):
                here = pl.ds(pl.multiple_of(r * ROWS + t * tok, tok), tok)
                so[yy, here, :] = result[:, t * tok : (t + 1) * tok].T.astype(BF16)
            return inner

        lax.fori_loop(0, rows // ROWS, chunk, 0)
        return carry

    def attend_and_send(s, carry):
        attend(s, 0)
        o_copy(s).start()
        return carry

    lax.fori_loop(1, SIDE, attend_and_send, 0)
    attend(0, 0)
    own_out = pltpu.make_async_copy(so.at[y], out.at[y], own_sem.at[4])
    own_out.start()

    def finish(owner):
        for a in range(2):
            head = owner * 2 + a
            lead = jnp.exp(lam[pl.ds(head, 1), :] * dist[2])
            raw = loc[head] + lead * dot(lq[head], in_recv[owner, a * hd : (a + 1) * hd, :], ((1,), (0,)))
            square = jnp.mean(raw * raw, axis=-1, keepdims=True)
            light[head] = (raw * lax.rsqrt(square + NORM_EPS) * gain[pl.ds(head, 1), :]).astype(BF16)

    own_in.wait()
    finish(h)

    def finish_from(i, carry):
        in_copy(i).wait_recv()
        finish(lax.rem(h + n_head - i, n_head))
        return carry

    lax.fori_loop(1, n_head, finish_from, 0)

    for d in range(1, SIDE):
        q_y(d).wait_send()
        kv_y(d).wait_send()
        o_copy(d).wait()
    own_out.wait()
    for d in range(SIDE):
        kv_pair(d).wait_send()
    kv_z().wait_send()
    for slot in (2, 0):
        for which in range(4):
            kv_x(slot, which).wait_send()
    for step in (1, 2):
        e_copy(step).wait_send()

    def drain(i, carry):
        state_copy(i).wait_send()
        in_copy(i).wait_send()
        return carry

    lax.fori_loop(1, n_head, drain, 0)


def mix(lq, lk, lv, sq, kvp, seg, lam, gain, n_head, n_ctx):
    heads, tok, hd = lq.shape
    rows = sq.shape[1]
    pack = kvp.shape[1]
    dma = pltpu.SemaphoreType.DMA
    vmem = pl.BlockSpec(memory_space=pltpu.VMEM)
    return pl.pallas_call(
        functools.partial(mix_kernel, n_head, n_ctx, hd ** (-0.5) * 1.4426950408889634),
        name="mix",
        out_shape=(
            jax.ShapeDtypeStruct((heads, tok, hd), BF16),
            jax.ShapeDtypeStruct((SIDE, rows, hd), BF16),
        ),
        in_specs=[vmem] * 8,
        out_specs=(vmem, vmem),
        scratch_shapes=[
            pltpu.VMEM((SIDE, rows, hd), BF16),
            pltpu.VMEM((3, SIDE, SIDE, pack, hd), BF16),
            pltpu.VMEM((SIDE, rows, hd), BF16),
            pltpu.VMEM((3 * SIDE * SIDE * tok, 2 * hd), BF16),
            pltpu.VMEM((3 * SIDE * SIDE + KEY_BLOCKS - 1, hd + ONES, tok), BF16),
            pltpu.VMEM((ROWS, 2 * hd), BF16),
            pltpu.VMEM((hd + ONES, ROWS), F32),
            pltpu.VMEM((tok, ROWS), F32),
            pltpu.VMEM((KEY_BLOCKS * tok, ROWS), F32),
            pltpu.VMEM((KEY_BLOCKS * tok, ROWS), F32),
            pltpu.VMEM((KEY_BLOCKS * tok, ROWS), BF16),
            pltpu.VMEM((KEY_BLOCKS * tok, ROWS), BF16),
            pltpu.VMEM((n_head, 2 * hd + 16, hd), BF16),
            pltpu.VMEM((n_head, 2 * hd + 16, hd), BF16),
            pltpu.VMEM((n_head, 2 * hd, hd), BF16),
            pltpu.VMEM((n_head, 2 * hd, hd), BF16),
            pltpu.VMEM((2 * hd + 8, hd), F32),
            pltpu.VMEM((2, 2 * hd + 8, hd), F32),
            pltpu.VMEM((heads, tok, hd), F32),
            pltpu.VMEM((3, tok, tok), F32),
            dma((SIDE,)),
            dma((SIDE,)),
            dma((SIDE,)),
            dma((SIDE,)),
            dma,
            dma,
            dma((8,)),
            dma((8,)),
            dma((SIDE,)),
            dma((SIDE,)),
            dma((n_head,)),
            dma((n_head,)),
            dma((2,)),
            dma((2,)),
            dma((n_head,)),
            dma((n_head,)),
            dma((SIDE,)),
            dma((SIDE,)),
            dma((5,)),
        ],
        compiler_params=pltpu.CompilerParams(collective_id=0, has_side_effects=True),
    )(lq, lk, lv, sq, kvp, seg, lam, gain)


def body(
    light_query,
    light_keys,
    light_values,
    decay_rate,
    norm_gain,
    soft_query,
    soft_keys,
    soft_values,
    segment_ids,
):
    n_head = lax.axis_size("head")
    n_ctx = lax.axis_size("ctx")
    tok, heads, hd = light_query.shape
    kv_heads = soft_keys.shape[1]

    def by_head(value):
        return jnp.transpose(value, (1, 0, 2))

    seg = segment_ids.astype(F32)[None, :]
    id_rows = jnp.broadcast_to(seg.astype(BF16)[None], (kv_heads, 16, tok))
    kvp = jnp.concatenate([by_head(soft_keys), jnp.transpose(soft_values, (1, 2, 0)), id_rows], axis=1)
    lam = jnp.broadcast_to(decay_rate[:, None], (heads, hd))
    sq = by_head(soft_query).reshape(kv_heads, heads // kv_heads * tok, hd)
    light, out = mix(
        by_head(light_query),
        by_head(light_keys),
        by_head(light_values),
        sq,
        kvp,
        seg,
        lam,
        norm_gain,
        n_head,
        n_ctx,
    )
    return (by_head(light), by_head(out.reshape(heads, tok, hd)))


def solution(mesh):
    wide = P(("ctx", "head"), None, None)
    return jax.shard_map(
        body,
        mesh=mesh,
        in_specs=(wide, wide, wide, P(), P(), wide, wide, wide, P(("ctx", "head"))),
        out_specs=(wide, wide),
        check_vma=False,
    )
```

```python
import functools

import jax
import jax.numpy as jnp
from jax import lax
from jax.experimental import pallas as pl
from jax.experimental.pallas import tpu as pltpu
from jax.sharding import PartitionSpec as P

NORM_EPS = 1e-06
FAR = -1e30
BIG = float(2**20)
F32 = jnp.float32
BF16 = jnp.bfloat16
SIDE = 4
KEY_BLOCKS = 4
ROWS = 512
ONES = 16
ENTER_AT = 0
FAR_AT = 2
MESH = pl.DeviceIdType.MESH


def dot(a, b, dims):
    return lax.dot_general(a, b, (dims, ((), ())), preferred_element_type=F32)


def two_terms(value):
    high = value.astype(BF16)
    low = (value - high.astype(F32)).astype(BF16)
    return high, low


def remote(src, dst, send, recv, **where):
    return pltpu.make_async_remote_copy(
        src_ref=src,
        dst_ref=dst,
        send_sem=send,
        recv_sem=recv,
        device_id=where,
        device_id_type=MESH,
    )


def mix_kernel(
    n_head,
    n_ctx,
    scale,
    lq,
    lk,
    lv,
    sq,
    ks,
    vs,
    seg,
    lam,
    gain,
    light,
    out,
    qg,
    kvw,
    so,
    keys,
    values,
    tagged,
    acc,
    score_d,
    score_a,
    score_b,
    prob_a,
    prob_b,
    peaks,
    kvp,
    st_send,
    st_recv,
    in_send,
    in_recv,
    e_send,
    e_recv,
    loc,
    dist,
    q_ss,
    q_rs,
    y_ss,
    y_rs,
    z_ss,
    z_rs,
    x_ss,
    x_rs,
    p_ss,
    p_rs,
    s_ss,
    s_rs,
    e_ss,
    e_rs,
    b_ss,
    b_rs,
    o_ss,
    o_rs,
    own_sem,
):
    tok = lq.shape[1]
    hd = lq.shape[2]
    c = lax.axis_index("ctx")
    h = lax.axis_index("head")
    x = lax.rem(h, SIDE)
    y = lax.div(h, SIDE)

    def ctx_at(step):
        return lax.rem(c + step + n_ctx, n_ctx)

    ids = seg[...].astype(F32)
    for g in range(SIDE):
        kvp[g, 0:tok, :] = ks[g]
        kvp[g, tok : 2 * tok, :] = vs[g]
        kvp[g, 2 * tok :, :] = jnp.broadcast_to(ids, (16, tok)).astype(BF16)

    barrier = pltpu.get_barrier_semaphore()
    for i in range(1, n_head):
        pl.semaphore_signal(
            barrier, inc=1, device_id={"head": lax.rem(h + i, n_head)}, device_id_type=MESH
        )
    for step in (1, -1, 2, -2):
        pl.semaphore_signal(barrier, inc=1, device_id={"ctx": ctx_at(step)}, device_id_type=MESH)
    pl.semaphore_wait(barrier, n_head - 1 + 4)

    def y_dev(d):
        return lax.rem(y + d, SIDE) * SIDE + x

    def x_dev(d):
        return y * SIDE + lax.rem(x + d, SIDE)

    def kv_y(d):
        to = lax.rem(y + d, SIDE)
        return remote(kvp.at[to], kvw.at[2, x, y], y_ss.at[d], y_rs.at[d], head=y_dev(d))

    def q_y(d):
        to = lax.rem(y + d, SIDE)
        return remote(sq.at[to], qg.at[y], q_ss.at[d], q_rs.at[d], head=y_dev(d))

    def kv_z():
        return remote(kvw.at[2, x], kvw.at[0, x], z_ss, z_rs, ctx=ctx_at(2))

    def kv_x(slot, which):
        at = slot // 2 * 4 + which
        half = SIDE // 2
        if which == 0:
            piece = kvw.at[slot, x]
            to = 1
        elif which == 1:
            piece = kvw.at[slot, x]
            to = SIDE - 1
        elif which == 2:
            piece = kvw.at[slot, lax.rem(x + SIDE - 1, SIDE), pl.ds(0, half)]
            to = 1
        else:
            piece = kvw.at[slot, lax.rem(x + 1, SIDE), pl.ds(half, half)]
            to = SIDE - 1
        return remote(piece, piece, x_ss.at[at], x_rs.at[at], head=x_dev(to))

    parity = lax.rem(c, 2)

    def kv_pair(d):
        at = lax.rem(x + d, SIDE)
        return remote(
            kvw.at[2 - 2 * parity, at],
            kvw.at[1, at],
            p_ss.at[d],
            p_rs.at[d],
            ctx=c + 1 - 2 * parity,
        )

    for d in range(1, SIDE):
        kv_y(d).start()
    own_kv = pltpu.make_async_copy(kvp.at[y], kvw.at[2, x, y], own_sem.at[0])
    own_kv.start()
    for d in (3, 2, 1):
        q_y(d).start()
    own_q = pltpu.make_async_copy(sq.at[y], qg.at[y], own_sem.at[1])
    own_q.start()

    row = lax.broadcasted_iota(jnp.int32, (tok, tok), 0)
    col = lax.broadcasted_iota(jnp.int32, (tok, tok), 1)
    seg_row = jnp.broadcast_to(ids, (tok, tok))
    seg_col = seg_row.T
    first = ids[:, 0:1]
    last = ids[:, tok - 1 : tok]
    dist[0] = jnp.where((row >= col) & (seg_row == seg_col), (col - row).astype(F32), FAR)
    dist[1] = jnp.where(seg_col == last, (row - (tok - 1)).astype(F32), FAR)
    dist[2] = jnp.where(seg_col == first, (-1 - row).astype(F32), FAR)
    edge = jnp.where(
        lax.broadcasted_iota(jnp.int32, (16, hd), 0) < 8,
        jnp.broadcast_to(first, (16, hd)),
        jnp.broadcast_to(last, (16, hd)),
    ).astype(BF16)

    def state_copy(i):
        to = lax.rem(h + i, n_head)
        return remote(st_send.at[to], st_recv.at[h], s_ss.at[i], s_rs.at[i], head=to)

    def make_state(i, carry):
        to = lax.rem(h + i, n_head)
        for a in range(2):
            head = to * 2 + a
            weighted = lk[head].astype(F32) * jnp.exp(lam[head] * dist[1])
            high, low = two_terms(weighted)
            values = lv[head]
            state = dot(high, values, ((0,), (0,))) + dot(low, values, ((0,), (0,)))
            st_send[to, a * hd : (a + 1) * hd, :] = state.astype(BF16)
        st_send[to, 2 * hd :, :] = edge
        return carry

    lax.fori_loop(1, n_head + 1, make_state, 0)
    own_state = pltpu.make_async_copy(st_send.at[h], st_recv.at[h], own_sem.at[2])
    own_state.start()

    for d in range(1, SIDE):
        kv_y(d).wait_recv()
    own_kv.wait()
    kv_z().start()
    kv_x(2, 0).start()
    kv_x(2, 1).start()

    def intra(head, carry):
        values = lv[head]
        scores = dot(lq[head], lk[head], ((1,), (1,)))
        high, low = two_terms(scores * jnp.exp(lam[head] * dist[0]))
        loc[head] = dot(high, values, ((1,), (0,))) + dot(low, values, ((1,), (0,)))
        return carry

    heads = lq.shape[0]
    lax.fori_loop(0, heads // 2, intra, 0, unroll=2)
    kv_x(2, 0).wait_recv()
    kv_x(2, 1).wait_recv()
    kv_x(2, 2).start()
    kv_x(2, 3).start()
    kv_z().wait_recv()
    kv_x(0, 0).start()
    kv_x(0, 1).start()
    kv_pair(0).start()
    def send_state(i, carry):
        state_copy(i).start()
        return carry

    lax.fori_loop(1, n_head, send_state, 0)
    lax.fori_loop(heads // 2, heads, intra, 0, unroll=2)

    def wait_state(i, carry):
        state_copy(i).wait_recv()
        return carry

    def powers(steps):
        return [jnp.exp(jnp.full((1, hd), -steps * lam[h * 2 + a], F32)) for a in range(2)]

    def edges_of(b):
        both = st_recv[b, 2 * hd :, :].astype(F32)
        return both[0:1], both[8:9]

    def step_on(block_rate, b, before, now):
        entry, end = edges_of(b)
        same = (before == end).astype(F32)
        after = tuple(
            st_recv[b, a * hd : (a + 1) * hd, :].astype(F32) + (same * block_rate[a]) * now[a]
            for a in range(2)
        )
        return end, after

    def e_copy(step):
        return remote(e_send, e_recv.at[step - 1], e_ss.at[step - 1], e_rs.at[step - 1], ctx=ctx_at(step))

    def in_copy(i):
        to = lax.rem(h + i, n_head)
        return remote(in_send.at[to], in_recv.at[h], b_ss.at[i], b_rs.at[i], head=to)

    own_in = pltpu.make_async_copy(in_send.at[h], in_recv.at[h], own_sem.at[3])

    def close_group():
        lax.fori_loop(1, n_head, wait_state, 0)
        own_state.wait()
        block_rate = powers(tok)
        zero = jnp.zeros((hd, hd), F32)
        nobody = jnp.full((1, hd), -1.0, F32)
        end, total = lax.fori_loop(
            0, n_head, lambda b, held: step_on(block_rate, b, held[0], held[1]), (nobody, (zero, zero))
        )
        for a in range(2):
            e_send[a * hd : (a + 1) * hd, :] = total[a]
        start, _ = edges_of(0)
        e_send[2 * hd :, :] = jnp.where(
            lax.broadcasted_iota(jnp.int32, (8, hd), 0) < 4,
            jnp.broadcast_to(start, (8, hd)),
            jnp.broadcast_to(end, (8, hd)),
        )

        e_copy(1).start()
        e_copy(2).start()

    def enter_group():
        block_rate = powers(tok)
        group_rate = powers(tok * n_head)
        e_copy(1).wait_recv()
        e_copy(2).wait_recv()

        near = e_recv[0, 2 * hd :, :]
        far = e_recv[1, 2 * hd :, :]
        near_start, near_end, far_end = near[0:1], near[4:5], far[4:5]
        through = ((near_start == near_end) & (near_end == far_end)).astype(F32)
        entering = tuple(
            e_recv[0, a * hd : (a + 1) * hd, :]
            + (through * group_rate[a]) * e_recv[1, a * hd : (a + 1) * hd, :]
            for a in range(2)
        )

        def give(b, held):
            before, now = held
            entry, _ = edges_of(b)
            linked = (before == entry).astype(F32)
            for a in range(2):
                in_send[b, a * hd : (a + 1) * hd, :] = (linked * now[a]).astype(BF16)
            return step_on(block_rate, b, before, now)

        lax.fori_loop(0, n_head, give, (near_end, entering))

        def send_in(i, carry):
            in_copy(i).start()
            return carry

        lax.fori_loop(1, n_head, send_in, 0)
        own_in.start()

    side = SIDE
    wide = KEY_BLOCKS * tok
    docs = lax.broadcasted_iota(jnp.int32, (hd, tok), 0).astype(F32)

    def tags(id_row):
        return (jnp.broadcast_to(id_row, (hd, tok)) == docs).astype(F32).T

    def lay(g):
        def lay_row(yy, carry):
            for xx in range(side):
                n = (g * side + yy) * side + xx
                at = pl.ds(pl.multiple_of(n * tok, tok), tok)
                id_row = kvw[g, xx, yy, 2 * tok :, :].astype(F32)[0:1]
                keys[at, 0:hd] = kvw[g, xx, yy, 0:tok, :]
                keys[at, hd:] = tags(id_row).astype(BF16)
                values[n, 0:hd, :] = kvw[g, xx, yy, tok : 2 * tok, :]
                values[n, hd:, :] = jnp.ones((ONES, tok), BF16)
            return carry

        lax.fori_loop(0, side, lay_row, 0)

    blocks = 3 * side * side
    for b in range(KEY_BLOCKS - 1):
        values[blocks + b] = jnp.zeros((hd + ONES, tok), BF16)
    acc[...] = jnp.zeros(acc.shape, F32)

    kv_x(2, 2).wait_recv()
    kv_x(2, 3).wait_recv()
    lay(2)
    own_q.wait()

    later_key = lax.broadcasted_iota(jnp.int32, (tok, ROWS), 0) > lax.rem(
        lax.broadcasted_iota(jnp.int32, (tok, ROWS), 1), tok
    )
    halves = qg.shape[1] // ROWS
    key_tiles = 2 * side * side // KEY_BLOCKS
    def o_copy(s):
        to = lax.rem(y + s, SIDE)
        return remote(so.at[to], out.at[y], o_ss.at[s], o_rs.at[s], head=y_dev(s))

    def place(k):
        s = lax.rem(1 + lax.div(k, halves), SIDE)
        r = lax.rem(k, halves)
        yy = lax.rem(y + s, SIDE)
        return s, r, yy, 2 * side * side + yy * side + x

    def attend(k, first_pass):
        s, r, yy, n = place(k)
        at = pl.ds(pl.multiple_of(r * ROWS, ROWS), ROWS)
        early = yy

        def first_block(i):
            return jnp.maximum(n - (i + 1) * KEY_BLOCKS, 0)

        def score(i):
            low = pl.multiple_of(first_block(i) * tok, tok)
            return dot(keys[pl.ds(low, wide), :], tagged[k], ((1,), (1,)))

        def fill(dst, i):
            found = score(i)
            dst[...] = found
            return jnp.max(found, axis=0, keepdims=True)

        def soften(src, dst, peak, highest):
            top = jnp.maximum(peak, highest)
            dst[...] = jnp.exp2((src[...] - top) * scale).astype(BF16)
            return top, jnp.exp2((peak - top) * scale)

        def gather(i, prob, fade):
            low = first_block(i)
            tile = jnp.concatenate([values[low + j] for j in range(KEY_BLOCKS)], axis=1)
            acc[k] = acc[k] * fade + dot(tile, prob[...], ((1,), (0,)))

        def turn(i, held):
            peak, fade, high = held
            gather(i - 1, prob_b, fade)
            peak, fade = soften(score_a, prob_b, peak, high)
            high = fill(score_a, i + 1)
            return peak, fade, high

        if first_pass:
            id_row = kvw[2, x, yy, 2 * tok :, :].astype(F32)[0:1]
            off = ((1.0 - tags(id_row)) * -BIG).astype(BF16)
            tagged[k, :, 0:hd] = qg[yy, at, :]
            for t in range(ROWS // tok):
                tagged[k, t * tok : (t + 1) * tok, hd:] = off
            diagonal = pl.ds(pl.multiple_of(n * tok, tok), tok)
            own_scores = dot(keys[diagonal, :], tagged[k], ((1,), (1,)))
            score_d[...] = jnp.where(later_key, -4.0 * BIG, own_scores)
            high = fill(score_a, 0)
            prob_b[tok:, :] = jnp.zeros((wide - tok, ROWS), BF16)
            peak = jnp.max(score_d[...], axis=0, keepdims=True)
            prob_b[0:tok, :] = jnp.exp2((score_d[...] - peak) * scale).astype(BF16)
            start = (peak, jnp.zeros((1, ROWS), F32), high)
            peak, fade, _ = lax.fori_loop(0, early, turn, start)
            gather(early - 1, prob_b, fade)
            peaks[k] = jnp.broadcast_to(peak, (8, ROWS))
            return

        high = fill(score_a, early)
        prob_b[...] = jnp.zeros(prob_b.shape, BF16)
        start = (peaks[k][0:1], jnp.ones((1, ROWS), F32), high)
        odd = lax.rem(early, 2)
        held = lax.fori_loop(early, early + odd, turn, start)
        _, fade, _ = lax.fori_loop(
            lax.div(early + odd, 2), key_tiles // 2, lambda p, now: turn(2 * p + 1, turn(2 * p, now)), held
        )
        gather(key_tiles - 1, prob_b, fade)
        result = acc[k, 0:hd, :] / acc[k, hd : hd + 1, :]
        for t in range(ROWS // tok):
            here = pl.ds(pl.multiple_of(r * ROWS + t * tok, tok), tok)
            so[yy, here, :] = result[:, t * tok : (t + 1) * tok].T.astype(BF16)

    def far_keys():
        kv_x(0, 0).wait_recv()
        kv_x(0, 1).wait_recv()
        kv_x(0, 2).start()
        kv_x(0, 3).start()
        kv_pair(SIDE - 1).start()
        kv_pair(1).start()

    def near_pass(turn, carry):
        k = lax.rem(turn + (SIDE - 1) * halves, SIDE * halves)
        s, r, _, _ = place(k)

        @pl.when((r == 0) & (s > 0))
        def _():
            q_y(SIDE - s).wait_recv()

        attend(k, True)
        pl.when(turn == FAR_AT)(far_keys)
        return carry

    lax.fori_loop(0, SIDE * halves, near_pass, 0)
    kv_x(0, 2).wait_recv()
    kv_x(0, 3).wait_recv()
    kv_pair(2).start()
    lay(0)
    for d in range(SIDE):
        kv_pair(d).wait_recv()
    lay(1)

    close_group()

    def far_pass(k, carry):
        attend(k, False)
        pl.when(k == ENTER_AT)(enter_group)
        s, r, _, _ = place(k)

        @pl.when((r == halves - 1) & (s > 0))
        def _():
            o_copy(s).start()

        return carry

    lax.fori_loop(0, SIDE * halves, far_pass, 0)
    own_out = pltpu.make_async_copy(so.at[y], out.at[y], own_sem.at[4])
    own_out.start()

    def finish(owner):
        for a in range(2):
            head = owner * 2 + a
            lead = jnp.exp(lam[head] * dist[2])
            raw = loc[head] + lead * dot(lq[head], in_recv[owner, a * hd : (a + 1) * hd, :], ((1,), (0,)))
            square = jnp.mean(raw * raw, axis=-1, keepdims=True)
            light[head] = (raw * lax.rsqrt(square + NORM_EPS) * gain[pl.ds(head, 1), :]).astype(BF16)

    own_in.wait()
    finish(h)

    def finish_from(i, carry):
        in_copy(i).wait_recv()
        finish(lax.rem(h + n_head - i, n_head))
        return carry

    lax.fori_loop(1, n_head, finish_from, 0)

    for d in range(1, SIDE):
        q_y(d).wait_send()
        kv_y(d).wait_send()
        o_copy(d).wait()
    own_out.wait()
    for d in range(SIDE):
        kv_pair(d).wait_send()
    kv_z().wait_send()
    for slot in (2, 0):
        for which in range(4):
            kv_x(slot, which).wait_send()
    for step in (1, 2):
        e_copy(step).wait_send()

    def drain(i, carry):
        state_copy(i).wait_send()
        in_copy(i).wait_send()
        return carry

    lax.fori_loop(1, n_head, drain, 0)


def mix(lq, lk, lv, sq, ks, vs, seg, lam, gain, n_head, n_ctx):
    heads, tok, hd = lq.shape
    rows = sq.shape[1]
    pack = 2 * tok + 16
    dma = pltpu.SemaphoreType.DMA
    vmem = pl.BlockSpec(memory_space=pltpu.VMEM)
    return pl.pallas_call(
        functools.partial(mix_kernel, n_head, n_ctx, hd ** (-0.5) * 1.4426950408889634),
        name="mix",
        out_shape=(
            jax.ShapeDtypeStruct((heads, tok, hd), BF16),
            jax.ShapeDtypeStruct((SIDE, rows, hd), BF16),
        ),
        in_specs=[vmem] * 3 + [pl.BlockSpec(memory_space=pl.ANY)] + [vmem] * 3 + [pl.BlockSpec(memory_space=pltpu.SMEM), vmem],
        out_specs=(vmem, vmem),
        scratch_shapes=[
            pltpu.VMEM((SIDE, rows, hd), BF16),
            pltpu.VMEM((3, SIDE, SIDE, pack, hd), BF16),
            pltpu.VMEM((SIDE, rows, hd), BF16),
            pltpu.VMEM((3 * SIDE * SIDE * tok, 2 * hd), BF16),
            pltpu.VMEM((3 * SIDE * SIDE + KEY_BLOCKS - 1, hd + ONES, tok), BF16),
            pltpu.VMEM((SIDE * rows // ROWS, ROWS, 2 * hd), BF16),
            pltpu.VMEM((SIDE * rows // ROWS, hd + ONES, ROWS), F32),
            pltpu.VMEM((tok, ROWS), F32),
            pltpu.VMEM((KEY_BLOCKS * tok, ROWS), F32),
            pltpu.VMEM((KEY_BLOCKS * tok, ROWS), F32),
            pltpu.VMEM((KEY_BLOCKS * tok, ROWS), BF16),
            pltpu.VMEM((KEY_BLOCKS * tok, ROWS), BF16),
            pltpu.VMEM((SIDE * rows // ROWS, 8, ROWS), F32),
            pltpu.VMEM((SIDE, pack, hd), BF16),
            pltpu.VMEM((n_head, 2 * hd + 16, hd), BF16),
            pltpu.VMEM((n_head, 2 * hd + 16, hd), BF16),
            pltpu.VMEM((n_head, 2 * hd, hd), BF16),
            pltpu.VMEM((n_head, 2 * hd, hd), BF16),
            pltpu.VMEM((2 * hd + 8, hd), F32),
            pltpu.VMEM((2, 2 * hd + 8, hd), F32),
            pltpu.VMEM((heads, tok, hd), F32),
            pltpu.VMEM((3, tok, tok), F32),
            dma((SIDE,)),
            dma((SIDE,)),
            dma((SIDE,)),
            dma((SIDE,)),
            dma,
            dma,
            dma((8,)),
            dma((8,)),
            dma((SIDE,)),
            dma((SIDE,)),
            dma((n_head,)),
            dma((n_head,)),
            dma((2,)),
            dma((2,)),
            dma((n_head,)),
            dma((n_head,)),
            dma((SIDE,)),
            dma((SIDE,)),
            dma((5,)),
        ],
        compiler_params=pltpu.CompilerParams(
            collective_id=0,
            has_side_effects=True,
        ),
    )(lq, lk, lv, sq, ks, vs, seg, lam, gain)


def body(
    light_query,
    light_keys,
    light_values,
    decay_rate,
    norm_gain,
    soft_query,
    soft_keys,
    soft_values,
    segment_ids,
):
    n_head = lax.axis_size("head")
    n_ctx = lax.axis_size("ctx")
    tok, heads, hd = light_query.shape
    kv_heads = soft_keys.shape[1]

    def by_head(value):
        return jnp.transpose(value, (1, 0, 2))

    seg = segment_ids[None, :]
    sq = by_head(soft_query).reshape(kv_heads, heads // kv_heads * tok, hd)
    light, out = mix(
        by_head(light_query),
        by_head(light_keys),
        by_head(light_values),
        sq,
        by_head(soft_keys),
        jnp.transpose(soft_values, (1, 2, 0)),
        seg,
        decay_rate,
        norm_gain,
        n_head,
        n_ctx,
    )
    return (by_head(light), by_head(out.reshape(heads, tok, hd)))


def solution(mesh):
    wide = P(("ctx", "head"), None, None)
    return jax.shard_map(
        body,
        mesh=mesh,
        in_specs=(wide, wide, wide, P(), P(), wide, wide, wide, P(("ctx", "head"))),
        out_specs=(wide, wide),
        check_vma=False,
    )
```
